32 devices in a mesh: segment: 8 (over y, x, core), head: 4 (over z).
Axes of the slice: x: 2, y: 2, z: 4, core: 2. Of those that a mesh axis runs over, the one named last changes fastest.
Arguments:
- grad_in: float32 [8, 128, 512], P('segment'), may hold values from -6 to 6
- memory: bfloat16 [8, 128, 512], P('segment'), may hold values from -120 to 120
- enc_grad_in: float32 [8, 128, 512], P('segment', None, 'head'), may hold values from -3 to 3
- act_stash: bfloat16 [8, 3, 128, 512], P('segment'), may hold values from -120 to 120
- slot_order: int32 [8, 3], P('segment'), may hold values from 0 to 2, each once within a row
- lengths: int32 [8, 3], P('segment'), may hold values from 16 to 128, as said below
- w_query: bfloat16 [8, 512, 4096], P('segment', None, 'head'), may hold values from -0.0234375 to 0.0234375
- w_key: bfloat16 [8, 512, 4096], P('segment', None, 'head'), may hold values from -0.25 to 0.25
- w_value: bfloat16 [8, 512, 4096], P('segment', None, 'head'), may hold values from -0.25 to 0.25
- w_out: bfloat16 [8, 4096, 512], P('segment', 'head'), may hold values from -0.09375 to 0.09375
Outputs:
- grad_out: float32 [8, 128, 512], P('segment')
- enc_grad_out: float32 [8, 128, 512], P('segment', None, 'head')
The draws below stay inside these ranges and needn't reach their ends.
Inputs may be any that keep to these rules, and one draw needn't show every extreme that they name: `slot_order`: each row lists every stash slot once. `lengths`: some entry equals 128.
All inputs are finite; a program needn't handle non-finite values.
Results may differ from the reference program's by a relative error of at most 0.018.
The reference program's roundings to bfloat16 on the way (of `decoded`, `queries`, `attention_low`, `context_grad`, `score_grad` and `query_grad`) count: a program that leaves them out, or rounds other values in their place, can miss the bound.
Values may be sent and summed in bfloat16 or wider, within the bound.
No kernel may reach another device: no remote copies, remote signals or barrier semaphores. Data moves between devices by JAX's collectives and lax.ppermute only.
A program may use at most 64 MiB of HBM per device.

```python
import jax
import jax.numpy as jnp
from jax import lax

D = 512
HEAD_DIM = 128
DEC_ROWS = 128
ENC_ROWS = 128
TICKS = 3
HEADS = 32
SEGMENTS = 8


def scaled_rows(key, shape):
    base = jnp.clip(jax.random.normal(key, shape, jnp.float32), -5.0, 5.0)
    return base.astype(jnp.bfloat16)


def draw_memory(key, part):
    return scaled_rows(jax.random.fold_in(key, 11), (SEGMENTS, ENC_ROWS, D))


def draw_act_stash(key, part):
    return scaled_rows(jax.random.fold_in(key, 13), (SEGMENTS, TICKS, DEC_ROWS, D))


def draw_lengths(key, part):
    drawn = jax.random.randint(jax.random.fold_in(key, 17), (SEGMENTS, TICKS), ENC_ROWS // 8, ENC_ROWS + 1, jnp.int32)
    return drawn.at[0, 0].set(ENC_ROWS)


def shard_levels(key, dims, shards, smallest, high):
    gain = 1.0
    for position, blocks in shards:
        steps = jax.random.uniform(jax.random.fold_in(jax.random.fold_in(key, 6), position), (blocks,), jnp.float32, smallest / len(shards), high / len(shards))
        gain = gain * jnp.repeat(jnp.exp(steps), dims[position] // blocks).reshape((-1,) + (1,) * (len(dims) - 1 - position))
    return gain


def centred(stream_key, shape, spread, reach, pieces=(), kind=jnp.bfloat16):
    entries = spread * jax.random.normal(stream_key, shape, jnp.float32)
    if pieces:
        entries = entries * shard_levels(stream_key, shape, pieces, -0.22, 0.18)
    return jnp.clip(entries, -reach, reach).astype(kind)


def setup_inputs(seed: int = 0) -> dict:
    seeds = jax.random.split(jax.random.key(seed), 11)
    grad_in = centred(seeds[0], (SEGMENTS, DEC_ROWS, D), 1.0, 6.0, ((0, 8),), jnp.float32)
    memory = draw_memory(jax.random.fold_in(seeds[10], 71), 0)
    enc_grad_in = centred(seeds[2], (SEGMENTS, ENC_ROWS, D), 0.5, 3.0, ((0, 8), (2, 4)), jnp.float32)
    act_stash = draw_act_stash(jax.random.fold_in(seeds[10], 71), 0)
    slot_order = jax.vmap(lambda own: jax.random.permutation(own, TICKS))(jax.random.split(seeds[4], SEGMENTS)).reshape((SEGMENTS, TICKS)).astype(jnp.int32)
    lengths = draw_lengths(jax.random.fold_in(seeds[10], 71), 0)
    w_query = centred(seeds[6], (SEGMENTS, D, HEADS * HEAD_DIM), (D * HEAD_DIM) ** -0.5, 0.0234375, ((0, 8), (2, 4)))
    w_key = centred(seeds[7], (SEGMENTS, D, HEADS * HEAD_DIM), D ** -0.5, 0.25, ((0, 8), (2, 4)))
    w_value = centred(seeds[8], (SEGMENTS, D, HEADS * HEAD_DIM), D ** -0.5, 0.25, ((0, 8), (2, 4)))
    w_out = centred(seeds[9], (SEGMENTS, HEADS * HEAD_DIM, D), (HEADS * HEAD_DIM) ** -0.5, 0.09375, ((0, 8), (1, 4)))
    return {"grad_in": grad_in, "memory": memory, "enc_grad_in": enc_grad_in, "act_stash": act_stash, "slot_order": slot_order, "lengths": lengths, "w_query": w_query, "w_key": w_key, "w_value": w_value, "w_out": w_out}


def widened(values):
    return lax.optimization_barrier(values.astype(jnp.bfloat16)).astype(jnp.float32)


def segment_terms(gradient, held, decoded, length, w_query, w_key, w_value, w_out):
    inner = w_query.shape[1]
    head_total = inner // HEAD_DIM
    dec_rows = decoded.shape[0]
    enc_rows = held.shape[0]
    queries = jnp.dot(decoded, w_query, preferred_element_type=jnp.float32).astype(jnp.bfloat16)
    keys = jnp.dot(held, w_key, preferred_element_type=jnp.float32).astype(jnp.bfloat16)
    values = jnp.dot(held, w_value, preferred_element_type=jnp.float32).astype(jnp.bfloat16)
    query_heads = queries.astype(jnp.float32).reshape(dec_rows, head_total, HEAD_DIM)
    key_heads = keys.astype(jnp.float32).reshape(enc_rows, head_total, HEAD_DIM)
    value_heads = values.astype(jnp.float32).reshape(enc_rows, head_total, HEAD_DIM)
    scores = jnp.einsum("qhd,khd->hqk", query_heads, key_heads)
    allowed = jnp.arange(enc_rows, dtype=jnp.int32)[None, None, :] < length
    scores = jnp.where(allowed, scores, jnp.float32(-1e30))
    row_max = jnp.max(scores, axis=-1, keepdims=True)
    expo = jnp.exp(scores - row_max)
    attention = expo / jnp.sum(expo, axis=-1, keepdims=True)
    attention_low = widened(attention)
    context_grad = jnp.dot(gradient.astype(jnp.bfloat16), w_out.T, preferred_element_type=jnp.float32)
    context_heads = widened(context_grad).reshape(dec_rows, head_total, HEAD_DIM)
    prob_grad = jnp.einsum("qhd,khd->hqk", context_heads, value_heads)
    score_grad = widened(attention * (prob_grad - jnp.sum(attention * prob_grad, axis=-1, keepdims=True)))
    query_grad = widened(jnp.einsum("hqk,khd->qhd", score_grad, key_heads)).reshape(dec_rows, inner)
    key_grad = widened(jnp.einsum("hqk,qhd->khd", score_grad, query_heads)).reshape(enc_rows, inner)
    value_grad = widened(jnp.einsum("hqk,qhd->khd", attention_low, context_heads)).reshape(enc_rows, inner)
    decoder_grad = jnp.dot(query_grad, w_query.astype(jnp.float32).T)
    memory_grad = jnp.dot(key_grad, w_key.astype(jnp.float32).T) + jnp.dot(value_grad, w_value.astype(jnp.float32).T)
    return decoder_grad, memory_grad


def reference(grad_in, memory, enc_grad_in, act_stash, slot_order, lengths, w_query, w_key, w_value, w_out):
    gradient = grad_in
    carried = enc_grad_in
    held = memory
    section_ids = jnp.arange(grad_in.shape[0], dtype=jnp.int32)
    for tick_index in range(TICKS):
        decoded = act_stash[section_ids, slot_order[:, tick_index].astype(jnp.int32)]

        def per_segment(operands):
            return segment_terms(*operands)

        decoder_grad, memory_grad = lax.map(per_segment, (gradient, held, decoded, lengths[:, tick_index], w_query, w_key, w_value, w_out))
        gradient = jnp.roll(gradient + decoder_grad, -1, axis=0)
        carried = jnp.roll(carried + memory_grad, -1, axis=0)
        if tick_index + 1 < TICKS:
            held = jnp.roll(held, -1, axis=0)
    return gradient, carried
```

```python
import jax
import jax.numpy as jnp
from jax import lax
from jax.experimental import pallas as pl
from jax.experimental.pallas import tpu as pltpu
from jax.sharding import PartitionSpec as P

HEAD_DIM = 128
TICKS = 3
LOW = jnp.bfloat16
FULL = jnp.float32


def dot(a, b, ca, cb):
    return lax.dot_general(a, b, (((ca,), (cb,)), ((), ())), preferred_element_type=FULL)


def cols(head):
    return slice(head * HEAD_DIM, (head + 1) * HEAD_DIM)


def tree_sum(terms):
    terms = list(terms)
    while len(terms) > 1:
        terms = [
            terms[i] + terms[i + 1] if i + 1 < len(terms) else terms[i]
            for i in range(0, len(terms), 2)
        ]
    return terms[0]


def project(decoded, held, length, wq, wk, wv, q_out, k_out, v_out, att_out):
    q_out[...] = dot(decoded, wq[...], 1, 0).astype(LOW)
    k_out[...] = dot(held, wk[...], 1, 0).astype(LOW)
    v_out[...] = dot(held, wv[...], 1, 0).astype(LOW)
    rows = held.shape[0]
    allowed = lax.broadcasted_iota(jnp.int32, (1, rows), 1) < length
    for head in range(q_out.shape[1] // HEAD_DIM):
        scores = dot(q_out[:, cols(head)], k_out[:, cols(head)], 1, 1)
        scores = jnp.where(allowed, scores, FULL(-1e30))
        expo = jnp.exp(scores - jnp.max(scores, axis=-1, keepdims=True))
        att_out[head] = expo * (1.0 / jnp.sum(expo, axis=-1, keepdims=True))


def chain(gradient, k_in, v_in, att, wq, wo, cg_out, sg_out, qg_tmp):
    cg_out[...] = dot(gradient.astype(LOW), wo[...], 1, 1).astype(LOW)
    for head in range(cg_out.shape[1] // HEAD_DIM):
        prob = dot(cg_out[:, cols(head)], v_in[:, cols(head)], 1, 1)
        weight = att[head]
        mean = jnp.sum(weight * prob, axis=-1, keepdims=True)
        sg_out[head] = (weight * (prob - mean)).astype(LOW)
        qg_tmp[:, cols(head)] = dot(sg_out[head], k_in[:, cols(head)], 1, 0).astype(LOW)
    return dot(qg_tmp[...], wq[...], 1, 1).astype(LOW)


def memory_terms(q_in, att, cg, sg, wk, wv, kg_tmp, vg_tmp):
    for head in range(cg.shape[1] // HEAD_DIM):
        kg_tmp[:, cols(head)] = dot(sg[head], q_in[:, cols(head)], 0, 0).astype(LOW)
        vg_tmp[:, cols(head)] = dot(att[head].astype(LOW), cg[:, cols(head)], 0, 0).astype(LOW)
    return dot(kg_tmp[...], wk[...], 1, 1) + dot(vg_tmp[...], wv[...], 1, 1)


def split(gradient):
    high = gradient.astype(LOW)
    return high, (gradient - high.astype(FULL)).astype(LOW)


def received(first, others, width):
    base = first[:, width : 2 * width].astype(FULL) + first[:, 2 * width : 3 * width].astype(FULL)
    parts = [first[:, :width].astype(FULL)] + [other[...].astype(FULL) for other in others]
    return base + tree_sum(parts)


def kernel(body, outs, scratch, smem, name):
    vmem = pl.BlockSpec(memory_space=pltpu.VMEM)
    scalar = pl.BlockSpec(memory_space=pltpu.SMEM)

    def call(*args):
        return pl.pallas_call(
            body,
            out_shape=[jax.ShapeDtypeStruct(shape, kind) for shape, kind in outs],
            in_specs=[scalar if i < smem else vmem for i in range(len(args))],
            out_specs=[vmem] * len(outs),
            scratch_shapes=[pltpu.VMEM(shape, kind) for shape, kind in scratch],
            name=name,
        )(*args)

    return call


def body(
    grad_in, memory, enc_grad_in, act_stash, slot_order, lengths, w_query, w_key, w_value, w_out
):
    segments = lax.axis_size("segment")
    groups = lax.axis_size("head")
    rows, width = grad_in.shape[1:]
    enc_rows = memory.shape[1]
    inner = w_query.shape[2]
    heads = inner // HEAD_DIM
    share = enc_grad_in.shape[2]
    wq, wk, wv, wo = w_query[0], w_key[0], w_value[0], w_out[0]
    stash, order, length = act_stash[0], slot_order, lengths
    mine = lax.axis_index("head").astype(jnp.int32).reshape(1)

    def send(value, k):
        pairs = [
            (s * groups + h, ((s - 1) % segments) * groups + (h ^ k))
            for s in range(segments)
            for h in range(groups)
        ]
        return lax.ppermute(value, ("segment", "head"), pairs)

    proj_outs = [
        ((rows, inner), LOW),
        ((enc_rows, inner), LOW),
        ((enc_rows, inner), LOW),
        ((heads, rows, enc_rows), FULL),
    ]
    chain_outs = [((rows, inner), LOW), ((heads, rows, enc_rows), LOW)]
    first_msg = ((rows, 4 * width), LOW)
    part_msg = ((rows, width), LOW)

    def write_first(msg, part_out, part, gradient, held):
        high, low = split(gradient)
        msg[:, :width] = part
        msg[:, width : 2 * width] = high
        msg[:, 2 * width : 3 * width] = low
        msg[:, 3 * width :] = held
        part_out[...] = part

    def open_body(
        order_ref, length_ref, g, mem, stash_ref, wq_, wk_, wv_, wo_,
        q, k, v, att, cg, sg, msg, part_out, tmp,
    ):
        project(stash_ref[order_ref[0, 0]], mem[...], length_ref[0, 0], wq_, wk_, wv_, q, k, v, att)
        part = chain(g[...], k, v, att, wq_, wo_, cg, sg, tmp)
        write_first(msg, part_out, part, g[...], mem[...])

    def fill_body(tick):
        def run(
            order_ref, length_ref, carry, q0, att0, cg, sg, first, stash_ref, wq_, wk_, wv_,
            q, k, v, att, carry_out, kg_tmp, vg_tmp,
        ):
            carry_out[...] = carry[...] + memory_terms(q0, att0, cg, sg, wk_, wv_, kg_tmp, vg_tmp)
            project(
                stash_ref[order_ref[0, tick]], first[:, 3 * width :], length_ref[0, tick],
                wq_, wk_, wv_, q, k, v, att,
            )

        return run

    def step_body(first, *refs):
        others, refs = refs[: groups - 1], refs[groups - 1 :]
        k, v, att, wq_, wo_, cg, sg, msg, part_out, tmp = refs
        gradient = received(first, others, width)
        part = chain(gradient, k, v, att, wq_, wo_, cg, sg, tmp)
        write_first(msg, part_out, part, gradient, first[:, 3 * width :])

    def last_body(mine_ref, first, *refs):
        others, refs = refs[: groups - 1], refs[groups - 1 :]
        carry, q, k, v, att, wq_, wk_, wv_, wo_ = refs[:9]
        msgs, (cg, sg, pieces, tmp, kg_tmp, vg_tmp) = refs[9 : 9 + groups], refs[9 + groups :]
        gradient = received(first, others, width)
        part = chain(gradient, k, v, att, wq_, wo_, cg, sg, tmp)
        total = carry[...] + memory_terms(q, att, cg, sg, wk_, wv_, kg_tmp, vg_tmp)
        for g in range(groups):
            pieces[g] = total[:, g * share : (g + 1) * share].astype(LOW)
        high, low = split(gradient)
        for j, msg in enumerate(msgs):
            base = 3 * width if j == 0 else width
            msg[:, :width] = part
            if j == 0:
                msg[:, width : 2 * width] = high
                msg[:, 2 * width : 3 * width] = low
            msg[:, base:] = pieces[mine_ref[0] ^ j]

    def close_body(first, *refs):
        others, (grad_out, enc_out) = refs[: groups - 1], refs[groups - 1 :]
        grad_out[...] = received(first, [other.at[:, :width] for other in others], width)
        pieces = [first[:, 3 * width :].astype(FULL)]
        pieces += [other[:, width:].astype(FULL) for other in others]
        enc_out[...] = tree_sum(pieces)

    grad_tmp = ((rows, inner), LOW)
    enc_tmp = ((enc_rows, inner), LOW)
    q, k, v, att, cg, sg, msg, part = kernel(
        open_body, proj_outs + chain_outs + [first_msg, part_msg], [grad_tmp], 2, "open"
    )(order, length, grad_in[0], memory[0], stash, wq, wk, wv, wo)
    carry = lax.dynamic_update_slice_in_dim(
        jnp.zeros((enc_rows, width), FULL), enc_grad_in[0], lax.axis_index("head") * share, 1
    )
    for tick in range(1, TICKS):
        others = [send(part, j) for j in range(groups - 1, 0, -1)][::-1]
        first = send(msg, 0)
        q, k, v, att, carry = kernel(
            fill_body(tick), proj_outs + [((enc_rows, width), FULL)], [enc_tmp] * 2, 2, "fill"
        )(order, length, carry, q, att, cg, sg, first, stash, wq, wk, wv)
        carry = send(carry, 0)
        if tick + 1 < TICKS:
            cg, sg, msg, part = kernel(
                step_body, chain_outs + [first_msg, part_msg], [grad_tmp], 0, "step"
            )(first, *others, k, v, att, wq, wo)
    msgs = kernel(
        last_body,
        [((rows, 3 * width + share), LOW)] + [((rows, width + share), LOW)] * (groups - 1),
        chain_outs + [((groups, enc_rows, share), LOW), grad_tmp, enc_tmp, enc_tmp],
        1,
        "last",
    )(mine, first, *others, carry, q, k, v, att, wq, wk, wv, wo)
    others = [send(msgs[j], j) for j in range(groups - 1, 0, -1)][::-1]
    first = send(msgs[0], 0)
    gradient, carried = kernel(
        close_body, [((rows, width), FULL), ((enc_rows, share), FULL)], [], 0, "close"
    )(first, *others)
    return (gradient[None], carried[None])


def solution(mesh):
    in_specs = (
        P("segment", None, None),
        P("segment", None, None),
        P("segment", None, "head"),
        P("segment", None, None, None),
        P("segment", None),
        P("segment", None),
        P("segment", None, "head"),
        P("segment", None, "head"),
        P("segment", None, "head"),
        P("segment", "head", None),
    )
    out_specs = (P("segment", None, None), P("segment", None, "head"))
    return jax.shard_map(body, mesh=mesh, in_specs=in_specs, out_specs=out_specs, check_vma=False)
```

```python
import jax
import jax.numpy as jnp
from jax import lax
from jax.experimental import pallas as pl
from jax.experimental.pallas import tpu as pltpu
from jax.sharding import PartitionSpec as P


HEAD_DIM = 128
LOW = jnp.bfloat16
FULL = jnp.float32
VMEM_LIMIT = 8 << 20


def dot(a, b, ca, cb):
    return lax.dot_general(a, b, (((ca,), (cb,)), ((), ())), preferred_element_type=FULL)


def cols(head):
    return slice(head * HEAD_DIM, (head + 1) * HEAD_DIM)


def tree_sum(terms):
    terms = list(terms)
    while len(terms) > 1:
        terms = [
            terms[i] + terms[i + 1] if i + 1 < len(terms) else terms[i]
            for i in range(0, len(terms), 2)
        ]
    return terms[0]


def project(decoded, held, allowed, wq, wk, wv, q_out, k_out, v_out, att_out):
    q_out[...] = dot(decoded, wq[...], 1, 0).astype(LOW)
    k_out[...] = dot(held, wk[...], 1, 0).astype(LOW)
    v_out[...] = dot(held, wv[...], 1, 0).astype(LOW)
    for head in range(q_out.shape[1] // HEAD_DIM):
        scores = dot(q_out[:, cols(head)], k_out[:, cols(head)], 1, 1)
        scores = jnp.where(allowed > 0, scores, FULL(-1e30))
        expo = jnp.exp(scores - jnp.max(scores, axis=-1, keepdims=True))
        att_out[head] = expo * (1.0 / jnp.sum(expo, axis=-1, keepdims=True))


def chain(gradient, k_in, v_in, att, wq, wo, cg_out, sg_out, qg_tmp):
    cg_out[...] = dot(gradient.astype(LOW), wo[...], 1, 1).astype(LOW)
    for head in range(cg_out.shape[1] // HEAD_DIM):
        prob = dot(cg_out[:, cols(head)], v_in[:, cols(head)], 1, 1)
        weight = att[head]
        mean = jnp.sum(weight * prob, axis=-1, keepdims=True)
        sg_out[head] = (weight * (prob - mean)).astype(LOW)
        qg_tmp[:, cols(head)] = dot(sg_out[head], k_in[:, cols(head)], 1, 0).astype(LOW)
    return dot(qg_tmp[...], wq[...], 1, 1).astype(LOW)


def memory_terms(q_in, att, cg, sg, wk, wv, kg_tmp, vg_tmp):
    for head in range(cg.shape[1] // HEAD_DIM):
        kg_tmp[:, cols(head)] = dot(sg[head], q_in[:, cols(head)], 0, 0).astype(LOW)
        vg_tmp[:, cols(head)] = dot(att[head].astype(LOW), cg[:, cols(head)], 0, 0).astype(LOW)
    return dot(kg_tmp[...], wk[...], 1, 1) + dot(vg_tmp[...], wv[...], 1, 1)


def split(gradient):
    high = gradient.astype(LOW)
    return high, (gradient - high.astype(FULL)).astype(LOW)


def received(first, others, width):
    base = first[:, width : 2 * width].astype(FULL) + first[:, 2 * width : 3 * width].astype(FULL)
    parts = [first[:, :width].astype(FULL)] + [other[...].astype(FULL) for other in others]
    return base + tree_sum(parts)


def kernel(body, outs, scratch, kinds=None, out_space=pltpu.VMEM):
    def call(*args):
        spaces = list(kinds) + [pltpu.VMEM] * (len(args) - len(kinds)) if kinds else [pltpu.VMEM] * len(args)
        args = [
            arg if space == pltpu.SMEM else pltpu.with_memory_space_constraint(arg, space)
            for arg, space in zip(args, spaces)
        ]
        return pl.pallas_call(
            body,
            out_shape=[out_space(shape, kind) for shape, kind in outs],
            in_specs=[pl.BlockSpec(memory_space=space) for space in spaces],
            out_specs=[pl.BlockSpec(memory_space=pltpu.VMEM)] * len(outs),
            scratch_shapes=scratch,
            compiler_params=pltpu.CompilerParams(vmem_limit_bytes=VMEM_LIMIT),
        )(*args)

    return call


def body(
    grad_in, memory, enc_grad_in, act_stash, slot_order, lengths, w_query, w_key, w_value, w_out
):
    segments = lax.axis_size("segment")
    groups = lax.axis_size("head")
    rows, width = grad_in.shape[1:]
    enc_rows = memory.shape[1]
    inner = w_query.shape[2]
    heads = inner // HEAD_DIM
    share = enc_grad_in.shape[2]
    ticks = act_stash.shape[1]
    mine = lax.axis_index("head").astype(jnp.int32).reshape(1)

    def send(value, k):
        pairs = [
            (s * groups + h, ((s - 1) % segments) * groups + (h ^ k))
            for s in range(segments)
            for h in range(groups)
        ]
        return lax.ppermute(value, ("segment", "head"), pairs)

    def exchange(first, part):
        head = send(first, 0)
        others = []
        for j in range(1, groups):
            others.append(send(part[j] if isinstance(part, list) else part, j))
        return head, others

    proj_outs = [
        ((rows, inner), LOW),
        ((enc_rows, inner), LOW),
        ((enc_rows, inner), LOW),
        ((heads, rows, enc_rows), FULL),
    ]
    chain_outs = [((rows, inner), LOW), ((heads, rows, enc_rows), LOW)]
    part_msg = ((rows, width), LOW)
    inner_tmp = pltpu.VMEM((rows, inner), LOW)
    held_at = slice(3 * width, 4 * width)
    carry_at = slice(4 * width, 5 * width)

    def write_first(msg, part_out, part, gradient, held):
        high, low = split(gradient)
        msg[:, :width] = part
        msg[:, width : 2 * width] = high
        msg[:, 2 * width : 3 * width] = low
        msg[:, held_at] = held
        part_out[...] = part

    def open_body(mine_ref, order_ref, length_ref, *refs):
        (stash, *hbm), refs = refs[:7], refs[7:]
        (q, att, cg, sg, msg, part_out, own, dec, allowed, *weights), refs = refs[:13], refs[13:]
        wq, wk, wv, wo = weights
        g, mem, k, v, tmp, sems = refs
        local = [wq, mem, wk, g, wo, wv]
        copies = [
            pltpu.make_async_copy(stash.at[0, order_ref[0, t]], dec.at[t], sems.at[len(local) + t])
            for t in range(ticks)
        ]
        copies += [
            pltpu.make_async_copy(src.at[0], dst, sems.at[i])
            for i, (src, dst) in enumerate(zip(hbm, local))
        ]
        for copy in copies:
            copy.start()
        positions = lax.broadcasted_iota(jnp.int32, (1, enc_rows), 1)
        for t in range(ticks):
            allowed[t : t + 1, :] = (positions < length_ref[0, t]).astype(FULL)
        heads_at = lax.broadcasted_iota(jnp.int32, own.shape, 1)
        own[...] = (heads_at == mine_ref[0]).astype(FULL)
        for copy in copies:
            copy.wait()
        project(dec[0], mem[...], allowed[0:1, :], wq, wk, wv, q, k, v, att)
        part = chain(g[...], k, v, att, wq, wo, cg, sg, tmp)
        write_first(msg, part_out, part, g[...], mem[...])

    def memory_open_body(own, enc, q, att, cg, sg, wk, wv, carry_out, kg_tmp, vg_tmp):
        total = memory_terms(q, att, cg, sg, wk, wv, kg_tmp, vg_tmp)
        for g in range(groups):
            at = slice(g * share, (g + 1) * share)
            carry_out[:, at] = (total[:, at] + enc[0] * own[0:1, g : g + 1]).astype(LOW)

    def memory_body(first, q, att, cg, sg, wk, wv, carry_out, kg_tmp, vg_tmp):
        total = memory_terms(q, att, cg, sg, wk, wv, kg_tmp, vg_tmp)
        carry_out[...] = first[:, carry_at].astype(FULL) + total

    def project_body(tick):
        def run(first, dec, allowed, wq, wk, wv, q, k, v, att):
            at = slice(tick, tick + 1)
            project(dec[tick], first[:, held_at], allowed[at, :], wq, wk, wv, q, k, v, att)

        return run

    def step_body(first, *refs):
        others, refs = refs[: groups - 1], refs[groups - 1 :]
        carry, k, v, att, wq, wo, cg, sg, msg, part_out, tmp = refs
        gradient = received(first, others, width)
        part = chain(gradient, k, v, att, wq, wo, cg, sg, tmp)
        write_first(msg, part_out, part, gradient, first[:, held_at])
        msg[:, carry_at] = carry[...]

    def last_body(mine_ref, first, *refs):
        others, refs = refs[: groups - 1], refs[groups - 1 :]
        carry, q, k, v, att, wq, wk, wv, wo = refs[:9]
        msgs, (cg, sg, pieces, tmp, kg_tmp, vg_tmp) = refs[9 : 9 + groups], refs[9 + groups :]
        gradient = received(first, others, width)
        part = chain(gradient, k, v, att, wq, wo, cg, sg, tmp)
        total = carry[...] + memory_terms(q, att, cg, sg, wk, wv, kg_tmp, vg_tmp)
        for g in range(groups):
            pieces[g] = total[:, g * share : (g + 1) * share].astype(LOW)
        high, low = split(gradient)
        for j, msg in enumerate(msgs):
            base = 3 * width if j == 0 else width
            msg[:, :width] = part
            if j == 0:
                msg[:, width : 2 * width] = high
                msg[:, 2 * width : 3 * width] = low
            msg[:, base:] = pieces[mine_ref[0] ^ j]

    def close_body(first, *refs):
        others, (grad_out, enc_out) = refs[: groups - 1], refs[groups - 1 :]
        grad_out[...] = received(first, [other.at[:, :width] for other in others], width)
        pieces = [first[:, 3 * width :].astype(FULL)]
        pieces += [other[:, width:].astype(FULL) for other in others]
        enc_out[...] = tree_sum(pieces)

    smem = pltpu.SMEM
    open_outs = proj_outs[:1] + proj_outs[3:] + chain_outs + [((rows, 4 * width), LOW), part_msg]
    open_outs += [((8, groups), FULL), (act_stash.shape[1:], LOW), ((8, enc_rows), FULL)]
    open_outs += [(w.shape[1:], LOW) for w in (w_query, w_key, w_value, w_out)]
    q, att, cg, sg, msg, part, own, dec, allowed, wq, wk, wv, wo = kernel(
        open_body,
        open_outs,
        [
            pltpu.VMEM((rows, width), FULL),
            pltpu.VMEM((enc_rows, width), LOW),
            pltpu.VMEM((enc_rows, inner), LOW),
            pltpu.VMEM((enc_rows, inner), LOW),
            inner_tmp,
            pltpu.SemaphoreType.DMA((6 + ticks,)),
        ],
        [smem] * 3 + [pltpu.HBM] * 7,
    )(mine, slot_order, lengths, act_stash, w_query, memory, w_key, grad_in, w_out, w_value)
    first, others = exchange(msg, part)
    (carry,) = kernel(memory_open_body, [((enc_rows, width), LOW)], [inner_tmp] * 2)(
        own, enc_grad_in, q, att, cg, sg, wk, wv
    )
    q, k, v, att = kernel(project_body(1), proj_outs, [])(first, dec, allowed, wq, wk, wv)
    cg, sg, msg, part = kernel(
        step_body, chain_outs + [((rows, 5 * width), LOW), part_msg], [inner_tmp]
    )(first, *others, carry, k, v, att, wq, wo)
    first, others = exchange(msg, part)
    (carry,) = kernel(memory_body, [((enc_rows, width), FULL)], [inner_tmp] * 2)(
        first, q, att, cg, sg, wk, wv
    )
    carry = send(carry, 0)
    q, k, v, att = kernel(project_body(2), proj_outs, [])(first, dec, allowed, wq, wk, wv)
    msgs = kernel(
        last_body,
        [((rows, 3 * width + share), LOW)] + [((rows, width + share), LOW)] * (groups - 1),
        [pltpu.VMEM(*shape) for shape in chain_outs]
        + [pltpu.VMEM((groups, enc_rows, share), LOW), inner_tmp, inner_tmp, inner_tmp],
        [smem],
    )(mine, first, *others, carry, q, k, v, att, wq, wk, wv, wo)
    first, others = exchange(msgs[0], list(msgs))
    gradient, carried = kernel(
        close_body, [((rows, width), FULL), ((enc_rows, share), FULL)], [],
        out_space=jax.ShapeDtypeStruct,
    )(first, *others)
    return (gradient[None], carried[None])


def solution(mesh):
    in_specs = (
        P("segment", None, None),
        P("segment", None, None),
        P("segment", None, "head"),
        P("segment", None, None, None),
        P("segment", None),
        P("segment", None),
        P("segment", None, "head"),
        P("segment", None, "head"),
        P("segment", None, "head"),
        P("segment", "head", None),
    )
    out_specs = (P("segment", None, None), P("segment", None, "head"))

    return jax.shard_map(body, mesh=mesh, in_specs=in_specs, out_specs=out_specs, check_vma=False)
```

```python
import jax
import jax.numpy as jnp
from jax import lax
from jax.experimental import pallas as pl
from jax.experimental.pallas import tpu as pltpu
from jax.sharding import PartitionSpec as P


HEAD_DIM = 128
LOW = jnp.bfloat16
FULL = jnp.float32
VMEM_LIMIT = 8 << 20


def dot(a, b, ca, cb):
    return lax.dot_general(a, b, (((ca,), (cb,)), ((), ())), preferred_element_type=FULL)


def cols(head):
    return slice(head * HEAD_DIM, (head + 1) * HEAD_DIM)


def tree_sum(terms):
    terms = list(terms)
    while len(terms) > 1:
        terms = [
            terms[i] + terms[i + 1] if i + 1 < len(terms) else terms[i]
            for i in range(0, len(terms), 2)
        ]
    return terms[0]


def project(decoded, held, allowed, wq, wk, wv, q_out, k_out, v_out, att_out, ready=None):
    ready = ready or (lambda name: None)
    ready("q")
    q_out[...] = dot(decoded[...], wq[...], 1, 0).astype(LOW)
    ready("k")
    k_out[...] = dot(held[...], wk[...], 1, 0).astype(LOW)
    ready("v")
    v_out[...] = dot(held[...], wv[...], 1, 0).astype(LOW)
    for head in range(q_out.shape[1] // HEAD_DIM):
        scores = dot(q_out[:, cols(head)], k_out[:, cols(head)], 1, 1)
        scores = jnp.where(allowed > 0, scores, FULL(-1e30))
        expo = jnp.exp(scores - jnp.max(scores, axis=-1, keepdims=True))
        att_out[head] = expo * (1.0 / jnp.sum(expo, axis=-1, keepdims=True))


def chain(gradient, k_in, v_in, att, wq, wo, cg_out, sg_out, qg_tmp):
    cg_out[...] = dot(gradient.astype(LOW), wo[...], 1, 1).astype(LOW)
    for head in range(cg_out.shape[1] // HEAD_DIM):
        prob = dot(cg_out[:, cols(head)], v_in[:, cols(head)], 1, 1)
        weight = att[head]
        mean = jnp.sum(weight * prob, axis=-1, keepdims=True)
        sg_out[head] = (weight * (prob - mean)).astype(LOW)
        qg_tmp[:, cols(head)] = dot(sg_out[head], k_in[:, cols(head)], 1, 0).astype(LOW)
    return dot(qg_tmp[...], wq[...], 1, 1).astype(LOW)


def memory_terms(q_in, att, cg, sg, wk, wv, kg_tmp, vg_tmp):
    for head in range(cg.shape[1] // HEAD_DIM):
        kg_tmp[:, cols(head)] = dot(sg[head], q_in[:, cols(head)], 0, 0).astype(LOW)
        vg_tmp[:, cols(head)] = dot(att[head].astype(LOW), cg[:, cols(head)], 0, 0).astype(LOW)
    return dot(kg_tmp[...], wk[...], 1, 1) + dot(vg_tmp[...], wv[...], 1, 1)


def chosen(flag, one, other):
    return jnp.where(flag > 0, one, other)


def halves(refs, width):
    terms = [ref[:, :width].astype(FULL) for ref in refs]
    return tree_sum(terms[0::2]), tree_sum(terms[1::2])


def joined(same, other, odd):
    return jnp.concatenate([chosen(odd, other, same), chosen(odd, same, other)], axis=1)


def kernel(body, outs, scratch, kinds=None, out_space=pltpu.VMEM):
    def call(*args):
        spaces = list(kinds) + [pltpu.VMEM] * (len(args) - len(kinds)) if kinds else [pltpu.VMEM] * len(args)
        args = [
            arg if space == pltpu.SMEM else pltpu.with_memory_space_constraint(arg, space)
            for arg, space in zip(args, spaces)
        ]
        return pl.pallas_call(
            body,
            out_shape=[out_space(shape, kind) for shape, kind in outs],
            in_specs=[pl.BlockSpec(memory_space=space) for space in spaces],
            out_specs=[pl.BlockSpec(memory_space=pltpu.VMEM)] * len(outs),
            scratch_shapes=scratch,
            compiler_params=pltpu.CompilerParams(vmem_limit_bytes=VMEM_LIMIT),
        )(*args)

    return call


def body(
    grad_in, memory, enc_grad_in, act_stash, slot_order, lengths, w_query, w_key, w_value, w_out
):
    segments = lax.axis_size("segment")
    groups = lax.axis_size("head")
    rows, width = grad_in.shape[1:]
    enc_rows = memory.shape[1]
    inner = w_query.shape[2]
    heads = inner // HEAD_DIM
    share = enc_grad_in.shape[2]
    ticks = act_stash.shape[1]
    mine = lax.axis_index("head").astype(jnp.int32).reshape(1)

    def send(value, k):
        pairs = [
            (s * groups + h, ((s - 1) % segments) * groups + (h ^ k))
            for s in range(segments)
            for h in range(groups)
        ]
        return lax.ppermute(value, ("segment", "head"), pairs)

    def sent_pair(value):
        pairs = [(h, h ^ 1) for h in range(groups)]
        return lax.ppermute(value, "head", pairs)

    half = width // 2
    proj_outs = [
        ((rows, inner), LOW),
        ((enc_rows, inner), LOW),
        ((enc_rows, inner), LOW),
        ((heads, rows, enc_rows), FULL),
    ]
    chain_outs = [((rows, inner), LOW), ((heads, rows, enc_rows), LOW)]
    pair_outs = [((rows, half), LOW), ((rows, half), FULL)]
    inner_tmp = pltpu.VMEM((rows, inner), LOW)

    def write_pair(part, base, odd, give, keep):
        left, right = part[:, :half], part[:, half:]
        give[...] = chosen(odd, left, right).astype(LOW)
        keep[...] = chosen(odd, right, left) + base

    def open_body(mine_ref, order_ref, length_ref, *refs):
        (stash, *hbm), refs = refs[:7], refs[7:]
        outs, refs = refs[:15], refs[15:]
        q, att, cg, sg, give, keep, own, flags, place, dec, allowed, wq, wk, wv, wo = outs
        g, mem, k, v, tmp, sems = refs
        local = [wq, mem, wk, wv, g, wo]
        turns = [
            pltpu.make_async_copy(stash.at[0, order_ref[0, t]], dec.at[t], sems.at[len(local) + t])
            for t in range(ticks)
        ]
        copies = [
            pltpu.make_async_copy(src.at[0], dst, sems.at[i])
            for i, (src, dst) in enumerate(zip(hbm, local))
        ]
        copies = turns[:1] + copies + turns[1:]
        for copy in copies:
            copy.start()
        waits = {"q": copies[:2], "k": copies[2:4], "v": copies[4:5]}

        def ready(name):
            for copy in waits[name]:
                copy.wait()

        positions = lax.broadcasted_iota(jnp.int32, (1, enc_rows), 1)
        for t in range(ticks):
            allowed[t : t + 1, :] = (positions < length_ref[0, t]).astype(FULL)
        own[...] = (lax.broadcasted_iota(jnp.int32, own.shape, 1) == mine_ref[0]).astype(FULL)
        flags[...] = jnp.broadcast_to((mine_ref[0] % 2).astype(FULL), flags.shape)
        columns = lax.broadcasted_iota(jnp.int32, place.shape, 1)
        start = (mine_ref[0] // 2) * share
        place[...] = ((columns >= start) & (columns < start + share)).astype(FULL)
        project(dec.at[0], mem, allowed[0:1, :], wq, wk, wv, q, k, v, att, ready)
        for copy in copies[5:]:
            copy.wait()
        odd = flags[0:1, 0:1]
        base = chosen(odd, g[:, half:], g[:, :half]) * place[0:1, :]
        write_pair(chain(g[...], k, v, att, wq, wo, cg, sg, tmp), base, odd, give, keep)

    def add_body(keep, got, place, small, first):
        total = keep[...] + got[...].astype(FULL)
        small[...] = total.astype(LOW)
        first[:, :half] = total.astype(LOW)
        rest = (total - total.astype(LOW).astype(FULL)) * place[0:1, :]
        first[:, half:] = sum(
            rest[:, j * share : (j + 1) * share] for j in range(groups // 2)
        ).astype(LOW)

    def memory_open_body(own, enc, q, att, cg, sg, wk, wv, carry_out, kg_tmp, vg_tmp):
        total = memory_terms(q, att, cg, sg, wk, wv, kg_tmp, vg_tmp)
        for g in range(groups):
            at = slice(g * share, (g + 1) * share)
            carry_out[:, at] = (total[:, at] + enc[0] * own[0:1, g : g + 1]).astype(LOW)

    def memory_body(carry, q, att, cg, sg, wk, wv, carry_out, kg_tmp, vg_tmp):
        total = memory_terms(q, att, cg, sg, wk, wv, kg_tmp, vg_tmp)
        carry_out[...] = (carry[...].astype(FULL) + total).astype(LOW)

    def memory_last_body(own, carry, q, att, cg, sg, wk, wv, *refs):
        outs, (kg_tmp, vg_tmp) = refs[:groups], refs[groups:]
        total = carry[...].astype(FULL) + memory_terms(q, att, cg, sg, wk, wv, kg_tmp, vg_tmp)
        pieces = [total[:, g * share : (g + 1) * share].astype(LOW) for g in range(groups)]
        for j, out in enumerate(outs):
            piece = pieces[0 ^ j]
            for g in range(1, groups):
                piece = jnp.where(own[0:1, g : g + 1] > 0, pieces[g ^ j], piece)
            out[...] = piece

    def project_body(tick):
        def run(held, dec, allowed, wq, wk, wv, q, k, v, att):
            at = slice(tick, tick + 1)
            project(dec.at[tick], held, allowed[at, :], wq, wk, wv, q, k, v, att)

        return run

    def gradient_of(refs, odd):
        same, other = halves(refs, half)
        return same, joined(same, other, odd)

    def step_body(*refs):
        msgs, refs = refs[:groups], refs[groups:]
        flags, place, k, v, att, wq, wo, cg, sg, give, keep, tmp = refs
        odd = flags[0:1, 0:1]
        same, gradient = gradient_of(msgs, odd)
        rest = jnp.concatenate([msgs[0][:, half:].astype(FULL)] * (groups // 2), axis=1)
        base = (same + rest) * place[0:1, :]
        write_pair(chain(gradient, k, v, att, wq, wo, cg, sg, tmp), base, odd, give, keep)

    def add_last_body(keep, got, *refs):
        pieces, msgs = refs[:groups], refs[groups:]
        total = (keep[...] + got[...].astype(FULL)).astype(LOW)
        for piece, msg in zip(pieces, msgs):
            msg[:, :half] = total
            msg[:, half:] = piece[...]

    def close_body(*refs):
        msgs, (flags, grad_out, enc_out) = refs[:groups], refs[groups:]
        grad_out[...] = gradient_of(msgs, flags[0:1, 0:1])[1]
        enc_out[...] = tree_sum([msg[:, half:].astype(FULL) for msg in msgs])

    smem = pltpu.SMEM
    open_outs = proj_outs[:1] + proj_outs[3:] + chain_outs + pair_outs
    open_outs += [((8, groups), FULL), ((8, 128), FULL), ((8, half), FULL)]
    open_outs += [(act_stash.shape[1:], LOW), ((8, enc_rows), FULL)]
    open_outs += [(w.shape[1:], LOW) for w in (w_query, w_key, w_value, w_out)]
    enc_low = ((enc_rows, width), LOW)
    msg_outs = [((rows, half), LOW), ((rows, half + share), LOW)]
    (q, att, cg, sg, give, keep, own, flags, place, dec, allowed, wq, wk, wv, wo) = kernel(
        open_body,
        open_outs,
        [
            pltpu.VMEM((rows, width), FULL),
            pltpu.VMEM((enc_rows, width), LOW),
            pltpu.VMEM((enc_rows, inner), LOW),
            pltpu.VMEM((enc_rows, inner), LOW),
            inner_tmp,
            pltpu.SemaphoreType.DMA((6 + ticks,)),
        ],
        [smem] * 3 + [pltpu.HBM] * 7,
    )(mine, slot_order, lengths, act_stash, w_query, memory, w_key, w_value, grad_in, w_out)
    held = memory[0]
    carry = None
    for tick in range(1, ticks):
        got = sent_pair(give)
        held = send(held, 0)
        (carry,) = kernel(
            memory_body if tick > 1 else memory_open_body, [enc_low], [inner_tmp] * 2
        )(*([carry] if tick > 1 else [own, enc_grad_in]), q, att, cg, sg, wk, wv)
        small, first = kernel(add_body, msg_outs, [])(keep, got, place)
        msgs = [send(small if j else first, j) for j in range(groups)]
        carry = send(carry, 0)
        q, k, v, att = kernel(project_body(tick), proj_outs, [])(held, dec, allowed, wq, wk, wv)
        cg, sg, give, keep = kernel(step_body, chain_outs + pair_outs, [inner_tmp])(
            *msgs, flags, place, k, v, att, wq, wo
        )
    got = sent_pair(give)
    pieces = kernel(
        memory_last_body, [((enc_rows, share), LOW)] * groups, [inner_tmp] * 2
    )(own, carry, q, att, cg, sg, wk, wv)
    outs = kernel(add_last_body, [((rows, half + share), LOW)] * groups, [])(keep, got, *pieces)
    msgs = [send(outs[j], j) for j in range(groups)]
    gradient, carried = kernel(
        close_body, [((rows, width), FULL), ((enc_rows, share), FULL)], [],
        out_space=jax.ShapeDtypeStruct,
    )(*msgs, flags)
    return (gradient[None], carried[None])


def solution(mesh):
    in_specs = (
        P("segment", None, None),
        P("segment", None, None),
        P("segment", None, "head"),
        P("segment", None, None, None),
        P("segment", None),
        P("segment", None),
        P("segment", None, "head"),
        P("segment", None, "head"),
        P("segment", None, "head"),
        P("segment", "head", None),
    )
    out_specs = (P("segment", None, None), P("segment", None, "head"))

    return jax.shard_map(body, mesh=mesh, in_specs=in_specs, out_specs=out_specs, check_vma=False)
```

```python
import jax
import jax.numpy as jnp
from jax import lax
from jax.experimental import pallas as pl
from jax.experimental.pallas import tpu as pltpu
from jax.sharding import PartitionSpec as P


HEAD_DIM = 128
LOW = jnp.bfloat16
FULL = jnp.float32
VMEM_LIMIT = 8 << 20


def dot(a, b, ca, cb):
    return lax.dot_general(a, b, (((ca,), (cb,)), ((), ())), preferred_element_type=FULL)


def cols(head):
    return slice(head * HEAD_DIM, (head + 1) * HEAD_DIM)


def tree_sum(terms):
    terms = list(terms)
    while len(terms) > 1:
        terms = [
            terms[i] + terms[i + 1] if i + 1 < len(terms) else terms[i]
            for i in range(0, len(terms), 2)
        ]
    return terms[0]


def attend(queries, keys, allowed, att_out):
    heads = range(queries.shape[1] // HEAD_DIM)
    scores = [dot(queries[:, cols(head)], keys[:, cols(head)], 1, 1) for head in heads]
    for head in heads:
        masked = jnp.where(allowed > 0, scores[head], FULL(-1e30))
        expo = jnp.exp(masked - jnp.max(masked, axis=-1, keepdims=True))
        att_out[head] = expo * (1.0 / jnp.sum(expo, axis=-1, keepdims=True))


def project(decoded, held, allowed, wq, wk, wv, q_out, k_out, v_out, att_out):
    queries = dot(decoded[...], wq[...], 1, 0).astype(LOW)
    keys = dot(held[...], wk[...], 1, 0).astype(LOW)
    q_out[...] = queries
    k_out[...] = keys
    v_out[...] = dot(held[...], wv[...], 1, 0).astype(LOW)
    attend(queries, keys, allowed, att_out)


def chain(context, k_in, v_in, att, wq, sg_out, qg_tmp):
    heads = range(context.shape[1] // HEAD_DIM)
    probs = [dot(context[:, cols(head)], v_in[:, cols(head)], 1, 1) for head in heads]
    grads = []
    for head in heads:
        weight = att[head]
        mean = jnp.sum(weight * probs[head], axis=-1, keepdims=True)
        grads.append((weight * (probs[head] - mean)).astype(LOW))
    for head in heads:
        sg_out[head] = grads[head]
        qg_tmp[:, cols(head)] = dot(grads[head], k_in[:, cols(head)], 1, 0).astype(LOW)
    return dot(qg_tmp[...], wq[...], 1, 1)


def context_of(gradient, wo, cg_out):
    context = dot(gradient.astype(LOW), wo[...], 1, 1).astype(LOW)
    cg_out[...] = context
    return context


def memory_terms(q_in, att, cg, sg, wk, wv, kg_tmp, vg_tmp):
    for head in range(cg.shape[1] // HEAD_DIM):
        kg_tmp[:, cols(head)] = dot(sg[head], q_in[:, cols(head)], 0, 0).astype(LOW)
        vg_tmp[:, cols(head)] = dot(att[head].astype(LOW), cg[:, cols(head)], 0, 0).astype(LOW)
    return dot(kg_tmp[...], wk[...], 1, 1) + dot(vg_tmp[...], wv[...], 1, 1)


def chosen(flag, one, other):
    return jnp.where(flag > 0, one, other)


def halves(refs, width):
    terms = [ref[:, :width].astype(FULL) for ref in refs]
    return tree_sum(terms[0::2]), tree_sum(terms[1::2])


def joined(same, other, odd):
    return jnp.concatenate([chosen(odd, other, same), chosen(odd, same, other)], axis=1)


def kernel(body, outs, scratch, kinds=None, out_space=pltpu.VMEM):
    def call(*args):
        spaces = list(kinds) + [pltpu.VMEM] * (len(args) - len(kinds)) if kinds else [pltpu.VMEM] * len(args)
        args = [
            arg if space == pltpu.SMEM else pltpu.with_memory_space_constraint(arg, space)
            for arg, space in zip(args, spaces)
        ]
        return pl.pallas_call(
            body,
            out_shape=[out_space(shape, kind) for shape, kind in outs],
            in_specs=[pl.BlockSpec(memory_space=space) for space in spaces],
            out_specs=[pl.BlockSpec(memory_space=pltpu.VMEM)] * len(outs),
            scratch_shapes=scratch,
            compiler_params=pltpu.CompilerParams(vmem_limit_bytes=VMEM_LIMIT),
        )(*args)

    return call


def body(
    grad_in, memory, enc_grad_in, act_stash, slot_order, lengths, w_query, w_key, w_value, w_out
):
    segments = lax.axis_size("segment")
    groups = lax.axis_size("head")
    rows, width = grad_in.shape[1:]
    enc_rows = memory.shape[1]
    inner = w_query.shape[2]
    heads = inner // HEAD_DIM
    share = enc_grad_in.shape[2]
    ticks = act_stash.shape[1]
    mine = lax.axis_index("head").astype(jnp.int32).reshape(1)

    def send(value, k):
        pairs = [
            (s * groups + h, ((s - 1) % segments) * groups + (h ^ k))
            for s in range(segments)
            for h in range(groups)
        ]
        return lax.ppermute(value, ("segment", "head"), pairs)

    def sent_pair(value):
        pairs = [(h, h ^ 1) for h in range(groups)]
        return lax.ppermute(value, "head", pairs)

    half = width // 2
    proj_outs = [
        ((rows, inner), LOW),
        ((enc_rows, inner), LOW),
        ((enc_rows, inner), LOW),
        ((heads, rows, enc_rows), FULL),
    ]
    chain_outs = [((rows, inner), LOW), ((heads, rows, enc_rows), LOW)]
    pair_outs = [((rows, half), LOW), ((rows, half), FULL)]
    inner_tmp = pltpu.VMEM((rows, inner), LOW)

    def write_pair(part, base, odd, give, keep):
        left, right = part[:, :half], part[:, half:]
        give[...] = chosen(odd, left, right).astype(LOW)
        keep[...] = chosen(odd, right, left) + base

    def open_body(mine_ref, *refs):
        (order_hbm, length_hbm, stash, *hbm), refs = refs[:9], refs[9:]
        outs, refs = refs[:15], refs[15:]
        q, att, cg, sg, give, keep, own, flags, place, dec, allowed, wk, wq, wv, wo = outs
        g, mem, k, v, tmp, order_ref, length_ref, sems = refs
        pairs = [(order_hbm, order_ref), (length_hbm, length_ref)]
        pairs += [(src.at[0], dst) for src, dst in zip(hbm, [mem, wk, wq, wv, g, wo])]
        copies = [
            pltpu.make_async_copy(src, dst, sems.at[i]) for i, (src, dst) in enumerate(pairs)
        ]
        for copy in copies:
            copy.start()
        order_at, length_at, mem_at, wk_at, wq_at, wv_at, g_at, wo_at = copies
        order_at.wait()
        turns = [
            pltpu.make_async_copy(stash.at[0, order_ref[0, t]], dec.at[t], sems.at[len(copies) + t])
            for t in range(ticks)
        ]
        for turn in turns:
            turn.start()
        own[...] = (lax.broadcasted_iota(jnp.int32, own.shape, 1) == mine_ref[0]).astype(FULL)
        flags[...] = jnp.broadcast_to((mine_ref[0] % 2).astype(FULL), flags.shape)
        columns = lax.broadcasted_iota(jnp.int32, place.shape, 1)
        start = (mine_ref[0] // 2) * share
        place[...] = ((columns >= start) & (columns < start + share)).astype(FULL)
        length_at.wait()
        positions = lax.broadcasted_iota(jnp.int32, (1, enc_rows), 1)
        for t in range(ticks):
            allowed[t : t + 1, :] = (positions < length_ref[0, t]).astype(FULL)
        mem_at.wait()
        wk_at.wait()
        keys = dot(mem[...], wk[...], 1, 0).astype(LOW)
        k[...] = keys
        turns[0].wait()
        wq_at.wait()
        queries = dot(dec[0], wq[...], 1, 0).astype(LOW)
        q[...] = queries
        attend(queries, keys, allowed[0:1, :], att)
        wv_at.wait()
        v[...] = dot(mem[...], wv[...], 1, 0).astype(LOW)
        g_at.wait()
        wo_at.wait()
        context = context_of(g[...], wo, cg)
        odd = flags[0:1, 0:1]
        base = chosen(odd, g[:, half:], g[:, :half]) * place[0:1, :]
        write_pair(chain(context, k, v, att, wq, sg, tmp), base, odd, give, keep)
        for turn in turns[1:]:
            turn.wait()

    def add_body(keep, got, place, small, first):
        total = keep[...] + got[...].astype(FULL)
        small[...] = total.astype(LOW)
        first[:, :half] = total.astype(LOW)
        rest = (total - total.astype(LOW).astype(FULL)) * place[0:1, :]
        first[:, half:] = sum(
            rest[:, j * share : (j + 1) * share] for j in range(groups // 2)
        ).astype(LOW)

    def memory_open_body(own, enc, q, att, cg, sg, wk, wv, carry_out, kg_tmp, vg_tmp):
        total = memory_terms(q, att, cg, sg, wk, wv, kg_tmp, vg_tmp)
        for g in range(groups):
            at = slice(g * share, (g + 1) * share)
            carry_out[:, at] = (total[:, at] + enc[0] * own[0:1, g : g + 1]).astype(LOW)

    def memory_body(carry, q, att, cg, sg, wk, wv, carry_out, kg_tmp, vg_tmp):
        total = memory_terms(q, att, cg, sg, wk, wv, kg_tmp, vg_tmp)
        carry_out[...] = (carry[...].astype(FULL) + total).astype(LOW)

    def memory_last_body(own, carry, q, att, cg, sg, wk, wv, *refs):
        outs, (kg_tmp, vg_tmp) = refs[:groups], refs[groups:]
        total = carry[...].astype(FULL) + memory_terms(q, att, cg, sg, wk, wv, kg_tmp, vg_tmp)
        pieces = [total[:, g * share : (g + 1) * share].astype(LOW) for g in range(groups)]
        for j, out in enumerate(outs):
            piece = pieces[0 ^ j]
            for g in range(1, groups):
                piece = jnp.where(own[0:1, g : g + 1] > 0, pieces[g ^ j], piece)
            out[...] = piece

    def project_body(tick):
        def run(held, dec, allowed, wq, wk, wv, q, k, v, att):
            at = slice(tick, tick + 1)
            project(dec.at[tick], held, allowed[at, :], wq, wk, wv, q, k, v, att)

        return run

    def gradient_of(refs, odd):
        same, other = halves(refs, half)
        return same, joined(same, other, odd)

    def step_body(*refs):
        msgs, refs = refs[:groups], refs[groups:]
        flags, place, k, v, att, wq, wo, cg, sg, give, keep, tmp = refs
        odd = flags[0:1, 0:1]
        same, gradient = gradient_of(msgs, odd)
        rest = jnp.concatenate([msgs[0][:, half:].astype(FULL)] * (groups // 2), axis=1)
        base = (same + rest) * place[0:1, :]
        part = chain(context_of(gradient, wo, cg), k, v, att, wq, sg, tmp)
        write_pair(part, base, odd, give, keep)

    def add_last_body(keep, got, *refs):
        pieces, msgs = refs[:groups], refs[groups:]
        total = (keep[...] + got[...].astype(FULL)).astype(LOW)
        for piece, msg in zip(pieces, msgs):
            msg[:, :half] = total
            msg[:, half:] = piece[...]

    def close_body(*refs):
        msgs, (flags, grad_out, enc_out) = refs[:groups], refs[groups:]
        grad_out[...] = gradient_of(msgs, flags[0:1, 0:1])[1]
        enc_out[...] = tree_sum([msg[:, half:].astype(FULL) for msg in msgs])

    smem = pltpu.SMEM
    open_outs = proj_outs[:1] + proj_outs[3:] + chain_outs + pair_outs
    open_outs += [((8, groups), FULL), ((8, 128), FULL), ((8, half), FULL)]
    open_outs += [(act_stash.shape[1:], LOW), ((8, enc_rows), FULL)]
    open_outs += [(w.shape[1:], LOW) for w in (w_key, w_query, w_value, w_out)]
    enc_low = ((enc_rows, width), LOW)
    msg_outs = [((rows, half), LOW), ((rows, half + share), LOW)]
    (q, att, cg, sg, give, keep, own, flags, place, dec, allowed, wk, wq, wv, wo) = kernel(
        open_body,
        open_outs,
        [
            pltpu.VMEM((rows, width), FULL),
            pltpu.VMEM((enc_rows, width), LOW),
            pltpu.VMEM((enc_rows, inner), LOW),
            pltpu.VMEM((enc_rows, inner), LOW),
            inner_tmp,
            pltpu.SMEM((1, ticks), jnp.int32),
            pltpu.SMEM((1, ticks), jnp.int32),
            pltpu.SemaphoreType.DMA((8 + ticks,)),
        ],
        [smem] + [pltpu.HBM] * 9,
    )(mine, slot_order, lengths, act_stash, memory, w_key, w_query, w_value, grad_in, w_out)
    held = memory[0]
    carry = None
    for tick in range(1, ticks):
        got = sent_pair(give)
        held = send(held, 0)
        (carry,) = kernel(
            memory_body if tick > 1 else memory_open_body, [enc_low], [inner_tmp] * 2
        )(*([carry] if tick > 1 else [own, enc_grad_in]), q, att, cg, sg, wk, wv)
        small, first = kernel(add_body, msg_outs, [])(keep, got, place)
        msgs = [send(small if j else first, j) for j in range(groups)]
        carry = send(carry, 0)
        q, k, v, att = kernel(project_body(tick), proj_outs, [])(held, dec, allowed, wq, wk, wv)
        cg, sg, give, keep = kernel(step_body, chain_outs + pair_outs, [inner_tmp])(
            *msgs, flags, place, k, v, att, wq, wo
        )
    got = sent_pair(give)
    pieces = kernel(
        memory_last_body, [((enc_rows, share), LOW)] * groups, [inner_tmp] * 2
    )(own, carry, q, att, cg, sg, wk, wv)
    outs = kernel(add_last_body, [((rows, half + share), LOW)] * groups, [])(keep, got, *pieces)
    msgs = [send(outs[j], j) for j in range(groups)]
    gradient, carried = kernel(
        close_body, [((rows, width), FULL), ((enc_rows, share), FULL)], [],
        out_space=jax.ShapeDtypeStruct,
    )(*msgs, flags)
    return (gradient[None], carried[None])


def solution(mesh):
    in_specs = (
        P("segment", None, None),
        P("segment", None, None),
        P("segment", None, "head"),
        P("segment", None, None, None),
        P("segment", None),
        P("segment", None),
        P("segment", None, "head"),
        P("segment", None, "head"),
        P("segment", None, "head"),
        P("segment", "head", None),
    )
    out_specs = (P("segment", None, None), P("segment", None, "head"))

    return jax.shard_map(body, mesh=mesh, in_specs=in_specs, out_specs=out_specs, check_vma=False)
```

```python
import jax
import jax.numpy as jnp
from jax import lax
from jax.experimental import pallas as pl
from jax.experimental.pallas import tpu as pltpu
from jax.sharding import PartitionSpec as P


HEAD_DIM = 128
LOW = jnp.bfloat16
FULL = jnp.float32
VMEM_LIMIT = 8 << 20


def dot(a, b, ca, cb):
    return lax.dot_general(a, b, (((ca,), (cb,)), ((), ())), preferred_element_type=FULL)


def cols(head):
    return slice(head * HEAD_DIM, (head + 1) * HEAD_DIM)


def tree_sum(terms):
    terms = list(terms)
    while len(terms) > 1:
        terms = [
            terms[i] + terms[i + 1] if i + 1 < len(terms) else terms[i]
            for i in range(0, len(terms), 2)
        ]
    return terms[0]


def attend(queries, keys, allowed, att_out, first=0):
    heads = range(queries.shape[1] // HEAD_DIM)
    scores = [dot(queries[:, cols(head)], keys[:, cols(head)], 1, 1) for head in heads]
    for head in heads:
        masked = jnp.where(allowed > 0, scores[head], FULL(-1e30))
        expo = jnp.exp(masked - jnp.max(masked, axis=-1, keepdims=True))
        att_out[first + head] = expo * (1.0 / jnp.sum(expo, axis=-1, keepdims=True))


def project(decoded, held, allowed, wq, wk, wv, q_out, k_out, v_out, att_out):
    queries = dot(decoded[...], wq[...], 1, 0).astype(LOW)
    keys = dot(held[...], wk[...], 1, 0).astype(LOW)
    q_out[...] = queries
    k_out[...] = keys
    v_out[...] = dot(held[...], wv[...], 1, 0).astype(LOW)
    attend(queries, keys, allowed, att_out)


def score_grads(context, keys, values, att, sg_out, qg_tmp, first=0):
    heads = range(context.shape[1] // HEAD_DIM)
    probs = [dot(context[:, cols(head)], values[:, cols(head)], 1, 1) for head in heads]
    grads = []
    for head in heads:
        weight = att[first + head]
        mean = jnp.sum(weight * probs[head], axis=-1, keepdims=True)
        grads.append((weight * (probs[head] - mean)).astype(LOW))
    for head in heads:
        sg_out[first + head] = grads[head]
        query_grad = dot(grads[head], keys[:, cols(head)], 1, 0)
        qg_tmp[:, cols(first + head)] = query_grad.astype(LOW)


def chain(context, k_in, v_in, att, wq, sg_out, qg_tmp):
    score_grads(context, k_in, v_in, att, sg_out, qg_tmp)
    return dot(qg_tmp[...], wq[...], 1, 1)


def context_of(gradient, wo, cg_out):
    context = dot(gradient.astype(LOW), wo[...], 1, 1).astype(LOW)
    cg_out[...] = context
    return context


def memory_terms(q_in, att, cg, sg, wk, wv, kg_tmp, vg_tmp):
    for head in range(cg.shape[1] // HEAD_DIM):
        kg_tmp[:, cols(head)] = dot(sg[head], q_in[:, cols(head)], 0, 0).astype(LOW)
        vg_tmp[:, cols(head)] = dot(att[head].astype(LOW), cg[:, cols(head)], 0, 0).astype(LOW)
    return dot(kg_tmp[...], wk[...], 1, 1) + dot(vg_tmp[...], wv[...], 1, 1)


def chosen(flag, one, other):
    return jnp.where(flag > 0, one, other)


def halves(refs, width):
    terms = [ref[:, :width].astype(FULL) for ref in refs]
    return tree_sum(terms[0::2]), tree_sum(terms[1::2])


def joined(same, other, odd):
    return jnp.concatenate([chosen(odd, other, same), chosen(odd, same, other)], axis=1)


def kernel(body, outs, scratch, kinds=None, out_space=pltpu.VMEM):
    def call(*args):
        spaces = list(kinds) + [pltpu.VMEM] * (len(args) - len(kinds)) if kinds else [pltpu.VMEM] * len(args)
        args = [
            arg if space == pltpu.SMEM else pltpu.with_memory_space_constraint(arg, space)
            for arg, space in zip(args, spaces)
        ]
        return pl.pallas_call(
            body,
            out_shape=[out_space(shape, kind) for shape, kind in outs],
            in_specs=[pl.BlockSpec(memory_space=space) for space in spaces],
            out_specs=[pl.BlockSpec(memory_space=pltpu.VMEM)] * len(outs),
            scratch_shapes=scratch,
            compiler_params=pltpu.CompilerParams(vmem_limit_bytes=VMEM_LIMIT),
        )(*args)

    return call


def body(
    grad_in, memory, enc_grad_in, act_stash, slot_order, lengths, w_query, w_key, w_value, w_out
):
    segments = lax.axis_size("segment")
    groups = lax.axis_size("head")
    rows, width = grad_in.shape[1:]
    enc_rows = memory.shape[1]
    inner = w_query.shape[2]
    heads = inner // HEAD_DIM
    share = enc_grad_in.shape[2]
    ticks = act_stash.shape[1]
    mine = lax.axis_index("head").astype(jnp.int32).reshape(1)

    def send(value, k):
        pairs = [
            (s * groups + h, ((s - 1) % segments) * groups + (h ^ k))
            for s in range(segments)
            for h in range(groups)
        ]
        return lax.ppermute(value, ("segment", "head"), pairs)

    def sent_pair(value):
        pairs = [(h, h ^ 1) for h in range(groups)]
        return lax.ppermute(value, "head", pairs)

    half = width // 2
    proj_outs = [
        ((rows, inner), LOW),
        ((enc_rows, inner), LOW),
        ((enc_rows, inner), LOW),
        ((heads, rows, enc_rows), FULL),
    ]
    chain_outs = [((rows, inner), LOW), ((heads, rows, enc_rows), LOW)]
    pair_outs = [((rows, half), LOW), ((rows, half), FULL)]
    inner_tmp = pltpu.VMEM((rows, inner), LOW)

    def write_pair(part, base, odd, give, keep):
        left, right = part[:, :half], part[:, half:]
        give[...] = chosen(odd, left, right).astype(LOW)
        keep[...] = chosen(odd, right, left) + base

    def open_body(mine_ref, *refs):
        (order_hbm, length_hbm, stash, *hbm), refs = refs[:9], refs[9:]
        outs, refs = refs[:15], refs[15:]
        q, att, cg, sg, give, keep, own, flags, place, dec, allowed, wk, wq, wv, wo = outs
        g, mem, stash_in, tmp, order_ref, length_ref, sems = refs
        g_hbm, mem_hbm, *weights_hbm = hbm
        count = iter(range(sems.shape[0]))

        def load(src, dst):
            return pltpu.make_async_copy(src, dst, sems.at[next(count)])

        small = [load(order_hbm, order_ref), load(length_hbm, length_ref)]
        small += [load(mem_hbm.at[0], mem), load(stash.at[0], stash_in)]
        wk_at, wq_at, wv_at, wo_at = [
            load(src.at[0], dst) for src, dst in zip(weights_hbm, (wk, wq, wv, wo))
        ]
        base_at = load(g_hbm.at[0], g)
        late = [wv_at, wo_at, base_at]
        for copy in [*small, wk_at, wq_at]:
            copy.start()
        for copy in late:
            copy.start()
        own[...] = (lax.broadcasted_iota(jnp.int32, own.shape, 1) == mine_ref[0]).astype(FULL)
        flags[...] = jnp.broadcast_to((mine_ref[0] % 2).astype(FULL), flags.shape)
        columns = lax.broadcasted_iota(jnp.int32, place.shape, 1)
        start = (mine_ref[0] // 2) * share
        place[...] = ((columns >= start) & (columns < start + share)).astype(FULL)
        for copy in small:
            copy.wait()
        positions = lax.broadcasted_iota(jnp.int32, (1, enc_rows), 1)
        for t in range(ticks):
            allowed[t : t + 1, :] = (positions < length_ref[0, t]).astype(FULL)
        for t in range(1, ticks):
            dec[t] = stash_in[order_ref[0, t]]
        decoded = stash_in[order_ref[0, 0]]
        held = mem[...]
        wk_at.wait()
        keys = dot(held, wk[...], 1, 0).astype(LOW)
        wq_at.wait()
        queries = dot(decoded, wq[...], 1, 0).astype(LOW)
        q[...] = queries
        attend(queries, keys, allowed[0:1, :], att)
        wv_at.wait()
        values = dot(held, wv[...], 1, 0).astype(LOW)
        base_at.wait()
        wo_at.wait()
        context = context_of(g[...], wo, cg)
        score_grads(context, keys, values, att, sg, tmp)
        odd = flags[0:1, 0:1]
        base = chosen(odd, g[:, half:], g[:, :half]) * place[0:1, :]
        write_pair(dot(tmp[...], wq[...], 1, 1), base, odd, give, keep)

    def add_body(keep, got, place, small, first):
        total = keep[...] + got[...].astype(FULL)
        small[...] = total.astype(LOW)
        first[:, :half] = total.astype(LOW)
        rest = (total - total.astype(LOW).astype(FULL)) * place[0:1, :]
        first[:, half:] = sum(
            rest[:, j * share : (j + 1) * share] for j in range(groups // 2)
        ).astype(LOW)

    def memory_open_body(own, enc, q, att, cg, sg, wk, wv, carry_out, kg_tmp, vg_tmp):
        total = memory_terms(q, att, cg, sg, wk, wv, kg_tmp, vg_tmp)
        for g in range(groups):
            at = slice(g * share, (g + 1) * share)
            carry_out[:, at] = (total[:, at] + enc[0] * own[0:1, g : g + 1]).astype(LOW)

    def memory_body(carry, q, att, cg, sg, wk, wv, carry_out, kg_tmp, vg_tmp):
        total = memory_terms(q, att, cg, sg, wk, wv, kg_tmp, vg_tmp)
        carry_out[...] = (carry[...].astype(FULL) + total).astype(LOW)

    def memory_last_body(own, carry, q, att, cg, sg, wk, wv, give, keep, kg_tmp, vg_tmp):
        total = carry[...].astype(FULL) + memory_terms(q, att, cg, sg, wk, wv, kg_tmp, vg_tmp)
        pieces = [total[:, g * share : (g + 1) * share] for g in range(groups)]
        for j in range(groups):
            piece = pieces[0 ^ j]
            for g in range(1, groups):
                piece = jnp.where(own[0:1, g : g + 1] > 0, pieces[g ^ j], piece)
            at = slice(j // 2 * share, (j // 2 + 1) * share)
            if j % 2:
                give[:, at] = piece.astype(LOW)
            else:
                keep[:, at] = piece

    def project_body(tick):
        def run(held, dec, allowed, wq, wk, wv, q, k, v, att):
            at = slice(tick, tick + 1)
            project(dec.at[tick], held, allowed[at, :], wq, wk, wv, q, k, v, att)

        return run

    def gradient_of(refs, odd):
        same, other = halves(refs, half)
        return same, joined(same, other, odd)

    def step_body(*refs):
        msgs, refs = refs[:groups], refs[groups:]
        flags, place, k, v, att, wq, wo, cg, sg, give, keep, tmp = refs
        odd = flags[0:1, 0:1]
        same, gradient = gradient_of(msgs, odd)
        rest = jnp.concatenate([msgs[0][:, half:].astype(FULL)] * (groups // 2), axis=1)
        base = (same + rest) * place[0:1, :]
        part = chain(context_of(gradient, wo, cg), k, v, att, wq, sg, tmp)
        write_pair(part, base, odd, give, keep)

    def add_half_body(keep, got, small):
        small[...] = (keep[...] + got[...].astype(FULL)).astype(LOW)

    def add_last_body(small, keep, got, *msgs):
        total = (keep[...] + got[...].astype(FULL)).astype(LOW)
        for j, msg in enumerate(msgs):
            msg[:, :half] = small[...]
            msg[:, half:] = total[:, j * share : (j + 1) * share]

    def close_body(*refs):
        msgs, (flags, grad_out, enc_out) = refs[:groups], refs[groups:]
        grad_out[...] = gradient_of(msgs, flags[0:1, 0:1])[1]
        enc_out[...] = tree_sum([msg[:, half:].astype(FULL) for msg in msgs[0::2]])

    smem = pltpu.SMEM
    open_outs = proj_outs[:1] + proj_outs[3:] + chain_outs + pair_outs
    open_outs += [((8, groups), FULL), ((8, 128), FULL), ((8, half), FULL)]
    open_outs += [(act_stash.shape[1:], LOW), ((8, enc_rows), FULL)]
    open_outs += [(w.shape[1:], LOW) for w in (w_key, w_query, w_value, w_out)]
    enc_low = ((enc_rows, width), LOW)
    msg_outs = [((rows, half), LOW), ((rows, half + share), LOW)]
    (q, att, cg, sg, give, keep, own, flags, place, dec, allowed, wk, wq, wv, wo) = kernel(
        open_body,
        open_outs,
        [
            pltpu.VMEM((rows, width), FULL),
            pltpu.VMEM((enc_rows, width), LOW),
            pltpu.VMEM(act_stash.shape[1:], LOW),
            inner_tmp,
            pltpu.SMEM((1, ticks), jnp.int32),
            pltpu.SMEM((1, ticks), jnp.int32),
            pltpu.SemaphoreType.DMA((16,)),
        ],
        [smem] + [pltpu.HBM] * 9,
    )(mine, slot_order, lengths, act_stash, grad_in, memory, w_key, w_query, w_value, w_out)
    held = memory[0]
    carry = None
    for tick in range(1, ticks):
        got = sent_pair(give)
        held = send(held, 0)
        (carry,) = kernel(
            memory_body if tick > 1 else memory_open_body, [enc_low], [inner_tmp] * 2
        )(*([carry] if tick > 1 else [own, enc_grad_in]), q, att, cg, sg, wk, wv)
        small, first = kernel(add_body, msg_outs, [])(keep, got, place)
        msgs = [send(small if j else first, j) for j in range(groups)]
        carry = send(carry, 0)
        q, k, v, att = kernel(project_body(tick), proj_outs, [])(held, dec, allowed, wq, wk, wv)
        cg, sg, give, keep = kernel(step_body, chain_outs + pair_outs, [inner_tmp])(
            *msgs, flags, place, k, v, att, wq, wo
        )
    got = sent_pair(give)
    enc_half = (enc_rows, groups // 2 * share)
    enc_give, enc_keep = kernel(
        memory_last_body, [(enc_half, LOW), (enc_half, FULL)], [inner_tmp] * 2
    )(own, carry, q, att, cg, sg, wk, wv)
    enc_got = sent_pair(enc_give)
    (small,) = kernel(add_half_body, [((rows, half), LOW)], [])(keep, got)
    wide = kernel(
        add_last_body, [((rows, half + share), LOW)] * (groups // 2), []
    )(small, enc_keep, enc_got)
    msgs = [send(small if j % 2 else wide[j // 2], j) for j in range(groups)]
    gradient, carried = kernel(
        close_body, [((rows, width), FULL), ((enc_rows, share), FULL)], [],
        out_space=jax.ShapeDtypeStruct,
    )(*msgs, flags)
    return (gradient[None], carried[None])


def solution(mesh):
    in_specs = (
        P("segment", None, None),
        P("segment", None, None),
        P("segment", None, "head"),
        P("segment", None, None, None),
        P("segment", None),
        P("segment", None),
        P("segment", None, "head"),
        P("segment", None, "head"),
        P("segment", None, "head"),
        P("segment", "head", None),
    )
    out_specs = (P("segment", None, None), P("segment", None, "head"))

    return jax.shard_map(body, mesh=mesh, in_specs=in_specs, out_specs=out_specs, check_vma=False)
```

```python
import jax
import jax.numpy as jnp
from jax import lax
from jax.experimental import pallas as pl
from jax.experimental.pallas import tpu as pltpu
from jax.sharding import PartitionSpec as P


HEAD_DIM = 128
LOW = jnp.bfloat16
FULL = jnp.float32
VMEM_LIMIT = 8 << 20


def dot(a, b, ca, cb):
    return lax.dot_general(a, b, (((ca,), (cb,)), ((), ())), preferred_element_type=FULL)


def cols(head):
    return slice(head * HEAD_DIM, (head + 1) * HEAD_DIM)


def tree_sum(terms):
    terms = list(terms)
    while len(terms) > 1:
        terms = [
            terms[i] + terms[i + 1] if i + 1 < len(terms) else terms[i]
            for i in range(0, len(terms), 2)
        ]
    return terms[0]


def attend(queries, keys, allowed, att_out, first=0):
    heads = range(queries.shape[1] // HEAD_DIM)
    scores = [dot(queries[:, cols(head)], keys[:, cols(head)], 1, 1) for head in heads]
    for head in heads:
        masked = jnp.where(allowed > 0, scores[head], FULL(-1e30))
        expo = jnp.exp(masked - jnp.max(masked, axis=-1, keepdims=True))
        att_out[first + head] = expo * (1.0 / jnp.sum(expo, axis=-1, keepdims=True))


def project(decoded, held, allowed, wq, wk, wv, q_out, k_out, v_out, att_out):
    queries = dot(decoded[...], wq[...], 1, 0).astype(LOW)
    keys = dot(held[...], wk[...], 1, 0).astype(LOW)
    q_out[...] = queries
    k_out[...] = keys
    v_out[...] = dot(held[...], wv[...], 1, 0).astype(LOW)
    attend(queries, keys, allowed, att_out)


def score_grads(context, keys, values, att, sg_out, qg_tmp, first=0):
    heads = range(context.shape[1] // HEAD_DIM)
    probs = [dot(context[:, cols(head)], values[:, cols(head)], 1, 1) for head in heads]
    grads = []
    for head in heads:
        weight = att[first + head]
        mean = jnp.sum(weight * probs[head], axis=-1, keepdims=True)
        grads.append((weight * (probs[head] - mean)).astype(LOW))
    for head in heads:
        sg_out[first + head] = grads[head]
        query_grad = dot(grads[head], keys[:, cols(head)], 1, 0)
        qg_tmp[:, cols(first + head)] = query_grad.astype(LOW)


def chain(context, k_in, v_in, att, wq, sg_out, qg_tmp):
    score_grads(context, k_in, v_in, att, sg_out, qg_tmp)
    return dot(qg_tmp[...], wq[...], 1, 1)


def context_of(gradient, wo, cg_out):
    context = dot(gradient.astype(LOW), wo[...], 1, 1).astype(LOW)
    cg_out[...] = context
    return context


def memory_terms(q_in, att, cg, sg, wk, wv, kg_tmp, vg_tmp):
    for head in range(cg.shape[1] // HEAD_DIM):
        kg_tmp[:, cols(head)] = dot(sg[head], q_in[:, cols(head)], 0, 0).astype(LOW)
        vg_tmp[:, cols(head)] = dot(att[head].astype(LOW), cg[:, cols(head)], 0, 0).astype(LOW)
    return dot(kg_tmp[...], wk[...], 1, 1) + dot(vg_tmp[...], wv[...], 1, 1)


def chosen(flag, one, other):
    return jnp.where(flag > 0, one, other)


def halves(refs, width):
    terms = [ref[:, :width].astype(FULL) for ref in refs]
    return tree_sum(terms[0::2]), tree_sum(terms[1::2])


def joined(same, other, odd):
    return jnp.concatenate([chosen(odd, other, same), chosen(odd, same, other)], axis=1)


def kernel(body, outs, scratch, kinds=None, out_space=pltpu.VMEM):
    def call(*args):
        spaces = list(kinds) + [pltpu.VMEM] * (len(args) - len(kinds)) if kinds else [pltpu.VMEM] * len(args)
        args = [
            arg if space == pltpu.SMEM else pltpu.with_memory_space_constraint(arg, space)
            for arg, space in zip(args, spaces)
        ]
        return pl.pallas_call(
            body,
            out_shape=[out_space(shape, kind) for shape, kind in outs],
            in_specs=[pl.BlockSpec(memory_space=space) for space in spaces],
            out_specs=[pl.BlockSpec(memory_space=pltpu.VMEM)] * len(outs),
            scratch_shapes=scratch,
            compiler_params=pltpu.CompilerParams(vmem_limit_bytes=VMEM_LIMIT),
        )(*args)

    return call


def body(
    grad_in, memory, enc_grad_in, act_stash, slot_order, lengths, w_query, w_key, w_value, w_out
):
    segments = lax.axis_size("segment")
    groups = lax.axis_size("head")
    rows, width = grad_in.shape[1:]
    enc_rows = memory.shape[1]
    inner = w_query.shape[2]
    heads = inner // HEAD_DIM
    share = enc_grad_in.shape[2]
    ticks = act_stash.shape[1]
    mine = lax.axis_index("head").astype(jnp.int32).reshape(1)

    def send(value, k):
        pairs = [
            (s * groups + h, ((s - 1) % segments) * groups + (h ^ k))
            for s in range(segments)
            for h in range(groups)
        ]
        return lax.ppermute(value, ("segment", "head"), pairs)

    def sent_pair(value, k=1):
        pairs = [(h, h ^ k) for h in range(groups)]
        return lax.ppermute(value, "head", pairs)

    half = width // 2
    near = groups // 2
    proj_outs = [
        ((rows, inner), LOW),
        ((enc_rows, inner), LOW),
        ((enc_rows, inner), LOW),
        ((heads, rows, enc_rows), FULL),
    ]
    chain_outs = [((rows, inner), LOW), ((heads, rows, enc_rows), LOW)]
    pair_outs = [((rows, half), LOW), ((rows, half), FULL)]
    inner_tmp = pltpu.VMEM((rows, inner), LOW)

    def write_pair(part, base, odd, give, keep):
        left, right = part[:, :half], part[:, half:]
        give[...] = chosen(odd, left, right).astype(LOW)
        keep[...] = chosen(odd, right, left) + base

    def open_body(mine_ref, *refs):
        (order_hbm, length_hbm, stash, *hbm), refs = refs[:9], refs[9:]
        outs, refs = refs[:15], refs[15:]
        q, att, cg, sg, give, keep, own, flags, place, dec, allowed, wk, wq, wv, wo = outs
        g, mem, stash_in, tmp, order_ref, length_ref, sems = refs
        g_hbm, mem_hbm, *weights_hbm = hbm
        count = iter(range(sems.shape[0]))

        def load(src, dst):
            return pltpu.make_async_copy(src, dst, sems.at[next(count)])

        small = [load(order_hbm, order_ref), load(length_hbm, length_ref)]
        small += [load(mem_hbm.at[0], mem), load(stash.at[0], stash_in)]
        wk_at, wq_at, wv_at, wo_at = [
            load(src.at[0], dst) for src, dst in zip(weights_hbm, (wk, wq, wv, wo))
        ]
        base_at = load(g_hbm.at[0], g)
        late = [wv_at, wo_at, base_at]
        for copy in [*small, wk_at, wq_at]:
            copy.start()
        for copy in late:
            copy.start(priority=1)
        own[...] = (lax.broadcasted_iota(jnp.int32, own.shape, 1) == mine_ref[0]).astype(FULL)
        flags[...] = jnp.broadcast_to((mine_ref[0] % 2).astype(FULL), flags.shape)
        columns = lax.broadcasted_iota(jnp.int32, place.shape, 1)
        start = (mine_ref[0] // 2) * share
        place[...] = ((columns >= start) & (columns < start + share)).astype(FULL)
        for copy in small:
            copy.wait()
        positions = lax.broadcasted_iota(jnp.int32, (1, enc_rows), 1)
        for t in range(ticks):
            allowed[t : t + 1, :] = (positions < length_ref[0, t]).astype(FULL)
        for t in range(1, ticks):
            dec[t] = stash_in[order_ref[0, t]]
        decoded = stash_in[order_ref[0, 0]]
        held = mem[...]
        wk_at.wait()
        keys = dot(held, wk[...], 1, 0).astype(LOW)
        wq_at.wait()
        queries = dot(decoded, wq[...], 1, 0).astype(LOW)
        q[...] = queries
        attend(queries, keys, allowed[0:1, :], att)
        wv_at.wait()
        values = dot(held, wv[...], 1, 0).astype(LOW)
        base_at.wait()
        wo_at.wait()
        context = context_of(g[...], wo, cg)
        score_grads(context, keys, values, att, sg, tmp)
        odd = flags[0:1, 0:1]
        base = chosen(odd, g[:, half:], g[:, :half]) * place[0:1, :]
        write_pair(dot(tmp[...], wq[...], 1, 1), base, odd, give, keep)

    def spread(rest, place):
        return jnp.concatenate([rest.astype(FULL)] * (groups // 2), axis=1) * place[0:1, :]

    def write_sum(total, place, carry, small, relay):
        small[...] = total.astype(LOW)
        rest = (total - total.astype(LOW).astype(FULL)) * place[0:1, :]
        relay[:, :width] = carry[...]
        relay[:, width:] = sum(
            rest[:, j * share : (j + 1) * share] for j in range(groups // 2)
        ).astype(LOW)

    def add_open_body(keep, got, place, carry, small, relay):
        write_sum(keep[...] + got[...].astype(FULL), place, carry, small, relay)

    def add_body(last, keep, got, place, carry, small, relay):
        total = keep[...] + got[...].astype(FULL) + spread(last[:, width:], place)
        write_sum(total, place, carry, small, relay)

    def memory_open_body(own, enc, q, att, cg, sg, wk, wv, carry_out, kg_tmp, vg_tmp):
        total = memory_terms(q, att, cg, sg, wk, wv, kg_tmp, vg_tmp)
        for g in range(groups):
            at = slice(g * share, (g + 1) * share)
            carry_out[:, at] = (total[:, at] + enc[0] * own[0:1, g : g + 1]).astype(LOW)

    def memory_body(carry, q, att, cg, sg, wk, wv, carry_out, kg_tmp, vg_tmp):
        total = memory_terms(q, att, cg, sg, wk, wv, kg_tmp, vg_tmp)
        carry_out[...] = (carry[:, :width].astype(FULL) + total).astype(LOW)

    def memory_last_body(own, carry, q, att, cg, sg, wk, wv, give, keep, kg_tmp, vg_tmp):
        total = memory_terms(q, att, cg, sg, wk, wv, kg_tmp, vg_tmp)
        total = carry[:, :width].astype(FULL) + total
        pieces = [total[:, g * share : (g + 1) * share] for g in range(groups)]
        for j in range(groups):
            piece = pieces[0 ^ j]
            for g in range(1, groups):
                piece = jnp.where(own[0:1, g : g + 1] > 0, pieces[g ^ j], piece)
            at = slice(j % near * share, (j % near + 1) * share)
            if j >= near:
                give[:, at] = piece.astype(LOW)
            else:
                keep[:, at] = piece

    def project_body(tick):
        def run(held, dec, allowed, wq, wk, wv, q, k, v, att):
            at = slice(tick, tick + 1)
            project(dec.at[tick], held, allowed[at, :], wq, wk, wv, q, k, v, att)

        return run

    def gradient_of(refs, odd):
        same, other = halves(refs, half)
        return same, joined(same, other, odd)

    def step_body(*refs):
        msgs, refs = refs[:groups], refs[groups:]
        flags, place, k, v, att, wq, wo, cg, sg, give, keep, tmp = refs
        odd = flags[0:1, 0:1]
        same, gradient = gradient_of(msgs, odd)
        base = same * place[0:1, :]
        part = chain(context_of(gradient, wo, cg), k, v, att, wq, sg, tmp)
        write_pair(part, base, odd, give, keep)

    def add_half_body(last, keep, got, place, small):
        total = keep[...] + got[...].astype(FULL) + spread(last[:, width:], place)
        small[...] = total.astype(LOW)

    def add_last_body(small, keep, got, *msgs):
        total = (keep[...] + got[...].astype(FULL)).astype(LOW)
        for j, msg in enumerate(msgs):
            msg[:, :half] = small[...]
            msg[:, half:] = total[:, j * share : (j + 1) * share]

    def close_body(*refs):
        msgs, (flags, grad_out, enc_out) = refs[:groups], refs[groups:]
        grad_out[...] = gradient_of(msgs, flags[0:1, 0:1])[1]
        enc_out[...] = tree_sum([msg[:, half:].astype(FULL) for msg in msgs[:near]])

    smem = pltpu.SMEM
    open_outs = proj_outs[:1] + proj_outs[3:] + chain_outs + pair_outs
    open_outs += [((8, groups), FULL), ((8, 128), FULL), ((8, half), FULL)]
    open_outs += [(act_stash.shape[1:], LOW), ((8, enc_rows), FULL)]
    open_outs += [(w.shape[1:], LOW) for w in (w_key, w_query, w_value, w_out)]
    enc_low = ((enc_rows, width), LOW)
    msg_outs = [((rows, half), LOW), ((enc_rows, width + share), LOW)]
    (q, att, cg, sg, give, keep, own, flags, place, dec, allowed, wk, wq, wv, wo) = kernel(
        open_body,
        open_outs,
        [
            pltpu.VMEM((rows, width), FULL),
            pltpu.VMEM((enc_rows, width), LOW),
            pltpu.VMEM(act_stash.shape[1:], LOW),
            inner_tmp,
            pltpu.SMEM((1, ticks), jnp.int32),
            pltpu.SMEM((1, ticks), jnp.int32),
            pltpu.SemaphoreType.DMA((16,)),
        ],
        [smem] + [pltpu.HBM] * 9,
    )(mine, slot_order, lengths, act_stash, grad_in, memory, w_key, w_query, w_value, w_out)
    held = memory[0]
    relay = None
    for tick in range(1, ticks):
        got = sent_pair(give)
        held = send(held, 0)
        (carry,) = kernel(
            memory_body if tick > 1 else memory_open_body, [enc_low], [inner_tmp] * 2
        )(*([relay] if tick > 1 else [own, enc_grad_in]), q, att, cg, sg, wk, wv)
        small, relay = kernel(add_body if tick > 1 else add_open_body, msg_outs, [])(
            *([relay] if tick > 1 else []), keep, got, place, carry
        )
        msgs = [send(small, j) for j in range(groups)]
        relay = send(relay, 0)
        q, k, v, att = kernel(project_body(tick), proj_outs, [])(held, dec, allowed, wq, wk, wv)
        cg, sg, give, keep = kernel(step_body, chain_outs + pair_outs, [inner_tmp])(
            *msgs, flags, place, k, v, att, wq, wo
        )
    got = sent_pair(give)
    enc_half = (enc_rows, groups // 2 * share)
    enc_give, enc_keep = kernel(
        memory_last_body, [(enc_half, LOW), (enc_half, FULL)], [inner_tmp] * 2
    )(own, relay, q, att, cg, sg, wk, wv)
    enc_got = sent_pair(enc_give, near)
    (small,) = kernel(add_half_body, [((rows, half), LOW)], [])(
        relay, keep, got, place
    )
    wide = kernel(
        add_last_body, [((rows, half + share), LOW)] * (groups // 2), []
    )(small, enc_keep, enc_got)
    msgs = [send(wide[j] if j < near else small, j) for j in range(groups)]
    gradient, carried = kernel(
        close_body, [((rows, width), FULL), ((enc_rows, share), FULL)], [],
        out_space=jax.ShapeDtypeStruct,
    )(*msgs, flags)
    return (gradient[None], carried[None])


def solution(mesh):
    in_specs = (
        P("segment", None, None),
        P("segment", None, None),
        P("segment", None, "head"),
        P("segment", None, None, None),
        P("segment", None),
        P("segment", None),
        P("segment", None, "head"),
        P("segment", None, "head"),
        P("segment", None, "head"),
        P("segment", "head", None),
    )
    out_specs = (P("segment", None, None), P("segment", None, "head"))

    return jax.shard_map(body, mesh=mesh, in_specs=in_specs, out_specs=out_specs, check_vma=False)
```
